32 devices in a mesh: row: 8 (over z, x), col: 4 (over y, core).
Axes of the slice: x: 2, y: 2, z: 4, core: 2. Of those that a mesh axis runs over, the one named last changes fastest.
Arguments:
- margin: bfloat16 [32, 128, 1152], P(('row', 'col')), may hold values from -0.2 to 1.2, as said below
- fock_matrix: bfloat16 [32, 128, 1152], P(('row', 'col')), may hold values from -0.4 to 0.4, as said below
- density: bfloat16 [32, 128, 1152], P(('row', 'col')), may hold values from -4 to 4, as said below
- present: int32 [32, 9], P(('row', 'col')), may hold values from 0 to 1, as said below
Outputs:
- gradient: float32 [32, 128, 1152], P(('row', 'col'))
- updated: float32 [32, 128, 1152], P(('row', 'col'))
The draws below stay inside these ranges and needn't reach their ends.
Inputs may be any that keep to these rules, and one draw needn't show every extreme that they name: present[r, 4] is 1; present[r, o + 4] equals present[r + o, 4 - o]; slots whose block lies outside the matrix are 0. `margin`: symmetric: block (r, o) is the transpose of block (r + o, -o); blocks where present is 0 are zero. `fock_matrix`: symmetric: block (r, o) is the transpose of block (r + o, -o); blocks where present is 0 are zero. `density`: symmetric: block (r, o) is the transpose of block (r + o, -o); blocks where present is 0 are zero.
All inputs are finite; a program needn't handle non-finite values.
Results may differ from the reference program's by a relative error of at most 0.0041.
Values may be sent and summed in bfloat16 or wider, within the bound.
A program may use at most 64 MiB of HBM per device.

```python
import jax
import jax.numpy as jnp
from jax import lax

BLOCK = 128
HALF_BAND = 4
BAND = 9
BLOCKS = 32


def pattern(key):
    random_bits = jax.random.randint(jax.random.fold_in(key, 11), (BLOCKS, HALF_BAND), 0, 4)
    upper_bits = (random_bits < 3).astype(jnp.int32)
    row_index = jnp.arange(BLOCKS, dtype=jnp.int32)
    columns = []
    for offset in range(-HALF_BAND, HALF_BAND + 1):
        if offset == 0:
            columns.append(jnp.ones((BLOCKS,), jnp.int32))
        elif offset > 0:
            columns.append(upper_bits[:, offset - 1] * (row_index + offset < BLOCKS).astype(jnp.int32))
        else:
            rolled = jnp.roll(upper_bits[:, -offset - 1], -offset)
            columns.append(rolled * (row_index + offset >= 0).astype(jnp.int32))
    return jnp.stack(columns, axis=1)


def symmetric(key, salt, factor):
    present = pattern(key)
    shape = (BLOCKS, BLOCK, BAND, BLOCK)
    random_draw = jnp.clip(jax.random.normal(jax.random.fold_in(key, salt), shape, jnp.float32), -4.0, 4.0)
    slot_list = []
    for offset in range(-HALF_BAND, HALF_BAND + 1):
        own_block = random_draw[:, :, HALF_BAND + offset, :]
        partner = jnp.roll(random_draw[:, :, HALF_BAND - offset, :], -offset, axis=0)
        slot_list.append(0.5 * (own_block + jnp.swapaxes(partner, 1, 2)))
    symmetrized = jnp.stack(slot_list, axis=2) * present.astype(jnp.float32)[:, None, :, None]
    return factor * symmetrized


def draw_present(key, part):
    return pattern(key)


def draw_margin(key, part):
    entry_scale = 0.4 * (BAND * BLOCK) ** (-0.5)
    values = symmetric(key, 21, entry_scale)
    identity = jnp.eye(BLOCK, dtype=jnp.float32)
    diagonal = jnp.zeros((BAND,), jnp.float32).at[HALF_BAND].set(1.0)
    values = values + identity[None, :, None, :] * diagonal[None, None, :, None]
    return values.reshape(BLOCKS, BLOCK, BAND * BLOCK).astype(jnp.bfloat16)


def draw_fock_matrix(key, part):
    entry_scale = (BAND * BLOCK) ** (-0.5)
    return symmetric(key, 33, entry_scale).reshape(BLOCKS, BLOCK, BAND * BLOCK).astype(jnp.bfloat16)


def draw_density(key, part):
    return symmetric(key, 45, 1.0).reshape(BLOCKS, BLOCK, BAND * BLOCK).astype(jnp.bfloat16)


def setup_inputs(seed: int = 0) -> dict:
    splits = jax.random.split(jax.random.key(seed), 5)
    margin = draw_margin(jax.random.fold_in(splits[4], 71), 0)
    fock_matrix = draw_fock_matrix(jax.random.fold_in(splits[4], 71), 0)
    density = draw_density(jax.random.fold_in(splits[4], 71), 0)
    present = draw_present(jax.random.fold_in(splits[4], 71), 0)
    return dict(margin=margin, fock_matrix=fock_matrix, density=density, present=present)


step_scale = 0.015625


def padded_rows(matrix, reach_rows):
    return jnp.pad(matrix, ((reach_rows, reach_rows), (0, 0), (0, 0)))


def band_product(left_band, right_wide, present):
    row_count = left_band.shape[0]
    block_size = left_band.shape[1]
    band_count = present.shape[1]
    half_band = (band_count - 1) // 2
    left_blocks = left_band.astype(jnp.float32).reshape(row_count, block_size, band_count, block_size)
    right_blocks = right_wide.astype(jnp.float32).reshape(right_wide.shape[0], block_size, band_count, block_size)
    accumulated = jnp.zeros((row_count, block_size, band_count, block_size), jnp.float32)
    for p in range(band_count):
        first_col = max(0, half_band - p)
        last_col = min(band_count, band_count + half_band - p)
        contribution = jnp.einsum("rik,rkqc->riqc", left_blocks[:, :, p, :], right_blocks[p:p + row_count, :, first_col:last_col, :], precision=lax.Precision.HIGHEST)
        accumulated = accumulated + jnp.pad(contribution, ((0, 0), (0, 0), (first_col + p - half_band, band_count - (last_col + p - half_band)), (0, 0)))
    keep_mask = present.astype(jnp.float32)[:, None, :, None]
    return (accumulated * keep_mask).reshape(row_count, block_size, band_count * block_size)


def band_mirror(wide, band_count):
    half_band = (band_count - 1) // 2
    block_size = wide.shape[1]
    row_count = wide.shape[0] - 2 * half_band
    wide_blocks = wide.reshape(wide.shape[0], block_size, band_count, block_size)
    slot_list = [jnp.swapaxes(wide_blocks[s:s + row_count, :, band_count - 1 - s, :], 1, 2) for s in range(band_count)]
    return jnp.stack(slot_list, axis=2).reshape(row_count, block_size, band_count * block_size)


def reference(margin, fock_matrix, density, present):
    band_count = present.shape[1]
    half_band = (band_count - 1) // 2
    margin_wide = padded_rows(margin, half_band)
    dens_over = band_product(density, margin_wide, present).astype(jnp.bfloat16)
    fock_dens = band_product(fock_matrix, padded_rows(dens_over, half_band), present).astype(jnp.bfloat16)
    gradient = fock_dens.astype(jnp.float32) - band_mirror(padded_rows(fock_dens, half_band), band_count).astype(jnp.float32)
    step_matrix = (-step_scale * gradient).astype(jnp.bfloat16)
    step_wide = padded_rows(step_matrix, half_band)
    first_term = band_product(dens_over, step_wide, present).astype(jnp.bfloat16)
    commuted = first_term.astype(jnp.float32) + band_mirror(padded_rows(first_term, half_band), band_count).astype(jnp.float32)
    commuted_half = commuted.astype(jnp.bfloat16)
    comm_over = band_product(commuted_half, margin_wide, present).astype(jnp.bfloat16)
    second_term = band_product(comm_over, step_wide, present).astype(jnp.bfloat16)
    second_mirror = band_mirror(padded_rows(second_term, half_band), band_count).astype(jnp.float32)
    updated = density.astype(jnp.float32) + commuted + 0.5 * (second_term.astype(jnp.float32) + second_mirror)
    return gradient, updated
```

```python
import functools

import jax
import jax.numpy as jnp
from jax import lax
from jax.experimental import pallas as pl
from jax.experimental.pallas import tpu as pltpu
from jax.sharding import PartitionSpec as P

STEP_SCALE = 0.015625


def runs(columns):
    out = []
    for j in sorted(columns):
        if out and out[-1][0] + out[-1][1] == j:
            out[-1] = (out[-1][0], out[-1][1] + 1)
        else:
            out.append((j, 1))
    return out


def receive_plan(half, parity):
    band = 2 * half + 1
    own = (half, half + 1)
    partner = 1 - 2 * parity
    owned = {}
    for i in range(band + 1):
        for j in range(i, band + 1):
            if j - i > half or i in own or j in own:
                continue
            chips = {i // 2 - half // 2, j // 2 - half // 2}
            rank = lambda e: (e != partner, e % 2 != 0, abs(e))
            owned.setdefault(min(chips, key=rank), []).append((i, j))
    plan = {}
    for e, pairs in owned.items():
        low = 2 * e + half
        options = []
        for pick in (0, 1):
            rows = {low: set(), low + 1: set()}
            for i, j in pairs:
                if i in rows and j in rows:
                    row = (i, j)[pick]
                    rows[row].add(i + j - row)
                elif i in rows:
                    rows[i].add(j)
                else:
                    rows[j].add(i)
            options.append({p: runs(c) for p, c in rows.items()})
        best = min(options, key=lambda o: sum(len(v) for v in o.values()))
        for p, v in best.items():
            plan[e, p] = v
    return plan


def kernel(ncol, n, b, half, margin, fock, density, kept, *rest):
    outs, rest = rest[:5], rest[5:]
    (dw, fw, sw, tw, zrow, xrow, trow, dv, fv, mv, gd, gt, gm, cf, ch, co, qd, qt, base, present,
     lsem, osem, wsend, wrecv, msend, mrecv) = rest
    band = 2 * half + 1
    r = lax.axis_index("row") * ncol + lax.axis_index("col")
    k = r // 2
    core = r % 2
    chips = n // 2
    parity = k % 2

    def device(t):
        return {"row": t // ncol, "col": t % ncol}

    def col(i, count=1):
        return pl.ds(pl.multiple_of(i * b, b), count * b)

    def valid_chip(e):
        return jnp.logical_and(k + e >= 0, k + e < chips)

    def valid(d):
        return jnp.logical_and(r + d >= 0, r + d < n)

    def both(x, y):
        return jnp.logical_and(x, y)

    sibling = device(r + 1 - 2 * core)
    offsets = [d for d in range(-half, half + 1) if d != 0]
    reach = half // 2
    hops = [e for m in range(reach, 0, -1) for e in (m, -m)]
    received = [receive_plan(half, q) for q in (0, 1)]

    loads = [
        pltpu.make_async_copy(density.at[0], dv, lsem.at[0]),
        pltpu.make_async_copy(fock.at[0], fv, lsem.at[1]),
        pltpu.make_async_copy(margin.at[0], mv, lsem.at[2]),
        pltpu.make_async_copy(kept, present, lsem.at[3]),
    ]
    for c in loads:
        c.start()

    barrier = pltpu.get_barrier_semaphore()
    for d in offsets:
        @pl.when(valid(d))
        def _():
            pl.semaphore_signal(barrier, inc=1, device_id=device(r + d),
                                device_id_type=pl.DeviceIdType.MESH)

    for e in hops:
        @pl.when(jnp.logical_not(valid_chip(e)))
        def _():
            p = half + 2 * e
            for w in (dw, fw, sw, tw):
                w[p * b:(p + 2) * b, :] = jnp.zeros((2 * b, w.shape[1]), w.dtype)
    for d in offsets:
        @pl.when(jnp.logical_not(valid(-d)))
        def _():
            for m in range(gm.shape[0]):
                gm[m, half - d] = jnp.zeros((b, b), gm.dtype)

    expected = jnp.minimum(r, half) + jnp.minimum(n - 1 - r, half)
    pl.semaphore_wait(barrier, expected)

    pending = []

    def reflect(w, sign, own_rows):
        middle = (half, half + 1)
        for q in (0, 1):
            known = {(p, j) for (_, p), v in received[q].items() for lo, count in v
                     for j in range(lo, lo + count)}
            todo = [(i, j) for i in range(band + 1) for j in range(band + 1)
                    if abs(i - j) <= half and i not in middle and (i, j) not in known
                    and (j in middle) == own_rows]

            def fill(todo=todo):
                for i, j in todo:
                    block = w[j * b:(j + 1) * b, (i + 1) * b:(i + 2) * b].T
                    w[i * b:(i + 1) * b, (j + 1) * b:(j + 2) * b] = block if sign > 0 else -block

            if own_rows:
                fill()
                return
            pl.when(parity == q)(fill)

    def spread_start(phase, own, w):
        here = pl.ds(pl.multiple_of((half + core) * b, b), b)
        share = pltpu.make_async_remote_copy(
            src_ref=own, dst_ref=w.at[here, col(core + 1, band)],
            send_sem=wsend.at[phase, 0], recv_sem=wrecv.at[phase, 0],
            device_id=sibling, device_id_type=pl.DeviceIdType.MESH)
        sends, relays = [], []
        for a, e in enumerate(hops):
            for q in (0, 1):
                for cc in (0, 1):
                    p = half - 2 * e + cc
                    for u, (lo, count) in enumerate(received[q].get((-e, p), [])):
                        slot = 1 + 2 * a + u
                        spot = w.at[p * b:(p + 1) * b, (lo + 1) * b:(lo + 1 + count) * b]
                        s0 = lo - p + half
                        send = pltpu.make_async_remote_copy(
                            src_ref=own.at[:, s0 * b:(s0 + count) * b], dst_ref=spot,
                            send_sem=wsend.at[phase, slot], recv_sem=wrecv.at[phase, slot],
                            device_id=device(r + 2 * e), device_id_type=pl.DeviceIdType.MESH)
                        relay = pltpu.make_async_remote_copy(
                            src_ref=spot, dst_ref=spot, send_sem=wsend.at[phase, 8 + slot],
                            recv_sem=wrecv.at[phase, 8 + slot], device_id=sibling,
                            device_id_type=pl.DeviceIdType.MESH)
                        out = both(both(core == cc, parity == (q + e) % 2), valid_chip(e))
                        back = both(both(core == cc, parity == q), valid_chip(-e))
                        theirs = both(both(core == 1 - cc, parity == q), valid_chip(-e))

                        @pl.when(out)
                        def _():
                            send.start()
                        sends.append((send, relay, out, back))
                        relays.append((relay, back, theirs))
        share.start()
        w[here, col(core + 1, band)] = own[...]
        return share, sends, relays

    def spread_finish(w, sign, flight, beside=None):
        share, sends, relays = flight
        share.wait_recv()
        reflect(w, sign, True)
        if beside is not None:
            beside()
        for send, relay, out, back in reversed(sends):
            @pl.when(back)
            def _():
                send.wait_recv()
                relay.start()
            pending.append((out, send))
        for relay, started, arriving in reversed(relays):
            @pl.when(arriving)
            def _():
                relay.wait_recv()
            pending.append((started, relay))
        pending.append((None, share))
        reflect(w, sign, False)

    def mirror(phase, left, w, own, m):
        copies = []
        for i, d in enumerate(sorted(offsets, key=lambda v: -abs(v))):
            product(left, w, own, (half + d,))
            c = pltpu.make_async_remote_copy(
                src_ref=own.at[:, (half + d) * b:(half + d + 1) * b],
                dst_ref=m.at[half - d], send_sem=msend.at[phase, i],
                recv_sem=mrecv.at[phase, i], device_id=device(r + d),
                device_id_type=pl.DeviceIdType.MESH)

            @pl.when(valid(d))
            def _():
                c.start()
            copies.append((d, c))
        product(left, w, own, (half,))
        m[half] = own[:, half * b:(half + 1) * b]
        for d, c in copies:
            pending.append((valid(d), c))
        return copies

    def mirror_wait(copies):
        for d, c in copies:
            @pl.when(valid(-d))
            def _():
                c.wait_recv()

    def product(left, w, out, columns=None):
        for c in columns or range(band):
            lo, hi = max(0, c - half), min(band, c + half + 1)
            rhs = w[pl.ds(pl.multiple_of((core + lo) * b, b), (hi - lo) * b), col(core + 1 + c)]
            acc = jnp.dot(left[:, lo * b:hi * b], rhs, preferred_element_type=jnp.float32)
            keep = present[0, c].astype(jnp.float32)
            out[:, c * b:(c + 1) * b] = (acc * keep).astype(out.dtype)

    stores = []

    def store(src):
        i = len(stores)
        c = pltpu.make_async_copy(src, outs[i].at[0], osem.at[i])
        c.start()
        stores.append(c)

    def body():
        loads[0].wait()
        dflight = spread_start(0, dv, dw)
        loads[1].wait()
        fflight = spread_start(1, fv, fw)
        loads[2].wait()
        loads[3].wait()
        sflight = spread_start(2, mv, sw)
        spread_finish(dw, 1, dflight)
        product(mv, dw, zrow)
        spread_finish(fw, 1, fflight)
        copies = mirror(0, zrow, fw, gd, gm.at[0])
        store(gd)
        mirror_wait(copies)
        for c in range(band):
            cols = slice(c * b, (c + 1) * b)
            other = gm[0, c].T
            gt[:, cols] = other
            g = other.astype(jnp.float32) - gd[:, cols].astype(jnp.float32)
            trow[:, cols] = (-STEP_SCALE * g).astype(trow.dtype)
        store(gt)
        tflight = spread_start(3, trow, tw)

        def beside():
            spread_finish(sw, 1, sflight)
            product(dv, sw, xrow)

        spread_finish(tw, -1, tflight, beside)
        copies = mirror(1, xrow, tw, cf, gm.at[1])
        mirror_wait(copies)
        for c in range(band):
            cols = slice(c * b, (c + 1) * b)
            v = cf[:, cols].astype(jnp.float32) + gm[1, c].T.astype(jnp.float32)
            ch[:, cols] = v.astype(ch.dtype)
            base[:, cols] = dv[:, cols].astype(jnp.float32) + v
        store(base)
        product(ch, sw, co)
        copies = mirror(2, co, tw, qd, gm.at[2])
        store(qd)
        mirror_wait(copies)
        for c in range(band):
            qt[:, c * b:(c + 1) * b] = gm[2, c].T
        store(qt)

    body()
    for c in stores:
        c.wait()
    for cond, c in pending:
        if cond is None:
            c.wait_send()
        else:
            @pl.when(cond)
            def _():
                c.wait_send()


def local(ncol, n, margin, fock_matrix, density, present):
    rows, b, width = margin.shape
    band = present.shape[1]
    half = (band - 1) // 2
    bf = jnp.bfloat16
    row = pltpu.VMEM((b, width), bf)
    wide = pltpu.VMEM(((band + 1) * b, (band + 3) * b), bf)
    out = jax.ShapeDtypeStruct((rows, b, width), bf)
    outs = pl.pallas_call(
        functools.partial(kernel, ncol, n, b, half),
        out_shape=(out, out, jax.ShapeDtypeStruct((rows, b, width), jnp.float32), out, out),
        in_specs=[pl.BlockSpec(memory_space=pltpu.HBM)] * 4,
        out_specs=[pl.BlockSpec(memory_space=pltpu.HBM)] * 5,
        scratch_shapes=[
            wide, wide, wide, wide, row, row, row, row, row, row,
            row, row, pltpu.VMEM((3, band, b, b), bf), row, row, row, row, row,
            pltpu.VMEM((b, width), jnp.float32), pltpu.SMEM((rows, band), jnp.int32),
            pltpu.SemaphoreType.DMA((4,)),
            pltpu.SemaphoreType.DMA((5,)),
            pltpu.SemaphoreType.DMA((4, 17)),
            pltpu.SemaphoreType.DMA((4, 17)),
            pltpu.SemaphoreType.DMA((3, 2 * half)),
            pltpu.SemaphoreType.DMA((3, 2 * half)),
        ],
        compiler_params=pltpu.CompilerParams(
            collective_id=0, has_side_effects=True, vmem_limit_bytes=67043328),
        name="density_step",
    )(margin, fock_matrix, density, present)
    gd, gt, base, qd, qt = (v.astype(jnp.float32) for v in outs)
    return gt - gd, base + 0.5 * (qd + qt)


def solution(mesh):
    nrow, ncol = mesh.shape["row"], mesh.shape["col"]
    spec3 = P(("row", "col"), None, None)
    return jax.shard_map(
        functools.partial(local, ncol, nrow * ncol), mesh=mesh,
        in_specs=(spec3, spec3, spec3, P(("row", "col"), None)),
        out_specs=(spec3, spec3), check_vma=False)
```

```python
import functools

import jax
import jax.numpy as jnp
from jax import lax
from jax.experimental import pallas as pl
from jax.experimental.pallas import tpu as pltpu
from jax.sharding import PartitionSpec as P

STEP_SCALE = 0.015625


def runs(columns):
    out = []
    for j in sorted(columns):
        if out and out[-1][0] + out[-1][1] == j:
            out[-1] = (out[-1][0], out[-1][1] + 1)
        else:
            out.append((j, 1))
    return out


def receive_plan(half, parity):
    band = 2 * half + 1
    own = (half, half + 1)
    partner = 1 - 2 * parity
    owned = {}
    for i in range(band + 1):
        for j in range(i, band + 1):
            if j - i > half or i in own or j in own:
                continue
            chips = {i // 2 - half // 2, j // 2 - half // 2}
            rank = lambda e: (e != partner, e % 2 != 0, abs(e))
            owned.setdefault(min(chips, key=rank), []).append((i, j))
    plan = {}
    for e, pairs in owned.items():
        low = 2 * e + half
        options = []
        for pick in (0, 1):
            rows = {low: set(), low + 1: set()}
            for i, j in pairs:
                if i in rows and j in rows:
                    row = (i, j)[pick]
                    rows[row].add(i + j - row)
                elif i in rows:
                    rows[i].add(j)
                else:
                    rows[j].add(i)
            options.append({p: runs(c) for p, c in rows.items()})
        best = min(options, key=lambda o: sum(len(v) for v in o.values()))
        for p, v in best.items():
            plan[e, p] = v
    return plan


def kernel(ncol, n, b, half, margin, fock, density, kept, *rest):
    outs, rest = rest[:5], rest[5:]
    gd, gt, base, qd, qt = (o.at[0] for o in outs)
    (dw, fw, sw, tw, zrow, xrow, trow, dv, fv, mv, gm, cf, ch, co, present,
     lsem, wsend, wrecv, msend, mrecv) = rest
    band = 2 * half + 1
    r = lax.axis_index("row") * ncol + lax.axis_index("col")
    k = r // 2
    core = r % 2
    chips = n // 2
    parity = k % 2

    def device(t):
        return {"row": t // ncol, "col": t % ncol}

    def col(i, count=1):
        return pl.ds(pl.multiple_of(i * b, b), count * b)

    def valid_chip(e):
        return jnp.logical_and(k + e >= 0, k + e < chips)

    def valid(d):
        return jnp.logical_and(r + d >= 0, r + d < n)

    def both(x, y):
        return jnp.logical_and(x, y)

    sibling = device(r + 1 - 2 * core)
    offsets = [d for d in range(-half, half + 1) if d != 0]
    reach = half // 2
    hops = [e for m in range(reach, 0, -1) for e in (m, -m)]
    received = [receive_plan(half, q) for q in (0, 1)]
    near = 2
    spots = len(hops) + near

    loads = [
        pltpu.make_async_copy(density.at[0], dv, lsem.at[0]),
        pltpu.make_async_copy(fock.at[0], fv, lsem.at[1]),
        pltpu.make_async_copy(margin.at[0], mv, lsem.at[2]),
        pltpu.make_async_copy(kept, present, lsem.at[3]),
    ]
    for c in loads:
        c.start()

    barrier = pltpu.get_barrier_semaphore()
    for d in offsets:
        @pl.when(valid(d))
        def _():
            pl.semaphore_signal(barrier, inc=1, device_id=device(r + d),
                                device_id_type=pl.DeviceIdType.MESH)

    for e in hops:
        @pl.when(jnp.logical_not(valid_chip(e)))
        def _():
            p = half + 2 * e
            for w in (dw, fw, sw, tw):
                w[p * b:(p + 2) * b, :] = jnp.zeros((2 * b, w.shape[1]), w.dtype)
    for d in offsets:
        @pl.when(jnp.logical_not(valid(-d)))
        def _():
            for m in range(gm.shape[0]):
                gm[m, half - d] = jnp.zeros((b, b), gm.dtype)

    expected = jnp.minimum(r, half) + jnp.minimum(n - 1 - r, half)
    pl.semaphore_wait(barrier, expected)

    pending = []

    def drain():
        for cond, c in pending:
            if cond is None:
                c.wait_send()
            else:
                pl.when(cond)(c.wait_send)
        pending.clear()

    def reflect(w, sign, own_rows):
        middle = (half, half + 1)
        for q in (0, 1):
            known = {(p, j) for (_, p), v in received[q].items() for lo, count in v
                     for j in range(lo, lo + count)}
            todo = [(i, j) for i in range(band + 1) for j in range(band + 1)
                    if abs(i - j) <= half and i not in middle and (i, j) not in known
                    and (j in middle) == own_rows]

            def fill(todo=todo):
                for i, j in todo:
                    block = w[j * b:(j + 1) * b, (i + 1) * b:(i + 2) * b].T
                    w[i * b:(i + 1) * b, (j + 1) * b:(j + 2) * b] = block if sign > 0 else -block

            if own_rows:
                fill()
                return
            pl.when(parity == q)(fill)

    def spread_plan(phase, own, w):
        here = pl.ds(pl.multiple_of((half + core) * b, b), b)
        share = pltpu.make_async_remote_copy(
            src_ref=own, dst_ref=w.at[here, col(core + 1, band)],
            send_sem=wsend.at[phase, 0], recv_sem=wrecv.at[phase, 0],
            device_id=sibling, device_id_type=pl.DeviceIdType.MESH)
        sends, relays = [], []
        for a, e in enumerate(hops):
            for q in (0, 1):
                for cc in (0, 1):
                    p = half - 2 * e + cc
                    for u, (lo, count) in enumerate(received[q].get((-e, p), [])):
                        slot = 1 + a + (len(hops) - near) * u
                        spot = w.at[p * b:(p + 1) * b, (lo + 1) * b:(lo + 1 + count) * b]
                        s0 = lo - p + half
                        send = pltpu.make_async_remote_copy(
                            src_ref=own.at[:, s0 * b:(s0 + count) * b], dst_ref=spot,
                            send_sem=wsend.at[phase, slot], recv_sem=wrecv.at[phase, slot],
                            device_id=device(r + 2 * e), device_id_type=pl.DeviceIdType.MESH)
                        relay = pltpu.make_async_remote_copy(
                            src_ref=spot, dst_ref=spot, send_sem=wsend.at[phase, spots + slot],
                            recv_sem=wrecv.at[phase, spots + slot], device_id=sibling,
                            device_id_type=pl.DeviceIdType.MESH)
                        out = both(both(core == cc, parity == (q + e) % 2), valid_chip(e))
                        back = both(both(core == cc, parity == q), valid_chip(-e))
                        theirs = both(both(core == 1 - cc, parity == q), valid_chip(-e))
                        sends.append((send, relay, out, back))
                        relays.append((relay, back, theirs))
        return share, sends, relays

    def spread_start(flight, w, own):
        share, sends, _ = flight
        here = pl.ds(pl.multiple_of((half + core) * b, b), b)
        for send, _, out, _ in sends:
            pl.when(out)(send.start)
        share.start()
        w[here, col(core + 1, band)] = own[...]

    def spread_finish(w, sign, flight):
        share, sends, relays = flight
        share.wait_recv()
        reflect(w, sign, True)
        for send, relay, out, back in reversed(sends):
            @pl.when(back)
            def _():
                send.wait_recv()
                relay.start()
            pending.append((out, send))
        for relay, started, arriving in reversed(relays):
            @pl.when(arriving)
            def _():
                relay.wait_recv()
            pending.append((started, relay))
        pending.append((None, share))
        reflect(w, sign, False)

    def mirror(phase, left, w, own, m):
        copies = []
        for i, d in enumerate(sorted(offsets, key=lambda v: -abs(v))):
            product(left, w, own, (half + d,))
            c = pltpu.make_async_remote_copy(
                src_ref=own.at[:, (half + d) * b:(half + d + 1) * b],
                dst_ref=m.at[half - d], send_sem=msend.at[phase, i],
                recv_sem=mrecv.at[phase, i], device_id=device(r + d),
                device_id_type=pl.DeviceIdType.MESH)

            @pl.when(valid(d))
            def _():
                c.start()
            copies.append((d, c))
        product(left, w, own, (half,))
        m[half] = own[:, half * b:(half + 1) * b]
        for d, c in copies:
            pending.append((valid(d), c))
        return copies

    def mirror_wait(copies):
        for d, c in copies:
            @pl.when(valid(-d))
            def _():
                c.wait_recv()

    def product(left, w, out, columns=None):
        for c in columns or range(band):
            lo, hi = max(0, c - half), min(band, c + half + 1)
            rhs = w[pl.ds(pl.multiple_of((core + lo) * b, b), (hi - lo) * b), col(core + 1 + c)]
            acc = jnp.dot(left[:, lo * b:hi * b], rhs, preferred_element_type=jnp.float32)
            keep = present[0, c].astype(jnp.float32)
            out[:, c * b:(c + 1) * b] = (acc * keep).astype(out.dtype)

    def body():
        dflight, fflight = spread_plan(0, dv, dw), spread_plan(1, fv, fw)
        sflight, tflight = spread_plan(2, mv, sw), spread_plan(0, trow, tw)
        loads[0].wait()
        spread_start(dflight, dw, dv)
        loads[1].wait()
        spread_start(fflight, fw, fv)
        loads[2].wait()
        loads[3].wait()
        spread_start(sflight, sw, mv)
        spread_finish(dw, 1, dflight)
        product(mv, dw, zrow)
        spread_finish(fw, 1, fflight)
        copies = mirror(0, zrow, fw, gd, gm.at[0])
        spread_finish(sw, 1, sflight)
        product(dv, sw, xrow)
        mirror_wait(copies)
        drain()
        for c in range(band):
            cols = slice(c * b, (c + 1) * b)
            other = gm[0, c].T
            gt[:, cols] = other
            g = other.astype(jnp.float32) - gd[:, cols].astype(jnp.float32)
            trow[:, cols] = (-STEP_SCALE * g).astype(trow.dtype)
        spread_start(tflight, tw, trow)

        spread_finish(tw, -1, tflight)
        copies = mirror(1, xrow, tw, cf, gm.at[1])
        mirror_wait(copies)
        drain()
        for c in range(band):
            cols = slice(c * b, (c + 1) * b)
            v = cf[:, cols].astype(jnp.float32) + gm[1, c].T.astype(jnp.float32)
            ch[:, cols] = v.astype(ch.dtype)
            base[:, cols] = dv[:, cols].astype(jnp.float32) + v
        product(ch, sw, co)
        copies = mirror(0, co, tw, qd, gm.at[2])
        mirror_wait(copies)
        for c in range(band):
            qt[:, c * b:(c + 1) * b] = gm[2, c].T

    body()
    drain()


def local(ncol, n, margin, fock_matrix, density, present):
    rows, b, width = margin.shape
    band = present.shape[1]
    half = (band - 1) // 2
    bf = jnp.bfloat16
    row = pltpu.VMEM((b, width), bf)
    wide = pltpu.VMEM(((band + 1) * b, (band + 3) * b), bf)
    out = jax.ShapeDtypeStruct((rows, b, width), bf)
    outs = pl.pallas_call(
        functools.partial(kernel, ncol, n, b, half),
        out_shape=(out, out, jax.ShapeDtypeStruct((rows, b, width), jnp.float32), out, out),
        in_specs=[pl.BlockSpec(memory_space=pltpu.HBM)] * 4,
        out_specs=[pl.BlockSpec(memory_space=pltpu.VMEM)] * 5,
        scratch_shapes=[
            wide, wide, wide, wide, row, row, row, row, row, row,
            pltpu.VMEM((3, band, b, b), bf), row, row, row, pltpu.SMEM((rows, band), jnp.int32),
            pltpu.SemaphoreType.DMA((4,)),
            pltpu.SemaphoreType.DMA((3, 5 + 2 * half)),
            pltpu.SemaphoreType.DMA((3, 5 + 2 * half)),
            pltpu.SemaphoreType.DMA((2, 2 * half)),
            pltpu.SemaphoreType.DMA((2, 2 * half)),
        ],
        compiler_params=pltpu.CompilerParams(
            collective_id=0, has_side_effects=True, vmem_limit_bytes=30000000),
        name="density_step",
    )(*(pltpu.with_memory_space_constraint(v, pltpu.HBM) for v in (margin, fock_matrix, density, present)))
    gd, gt, base, qd, qt = (v.astype(jnp.float32) for v in outs)
    return gt - gd, base + 0.5 * (qd + qt)


def solution(mesh):
    nrow, ncol = mesh.shape["row"], mesh.shape["col"]
    spec3 = P(("row", "col"), None, None)
    return jax.shard_map(
        functools.partial(local, ncol, nrow * ncol), mesh=mesh,
        in_specs=(spec3, spec3, spec3, P(("row", "col"), None)),
        out_specs=(spec3, spec3), check_vma=False)
```

```python
import functools

import jax
import jax.numpy as jnp
from jax import lax
from jax.experimental import pallas as pl
from jax.experimental.pallas import tpu as pltpu
from jax.sharding import PartitionSpec as P

STEP_SCALE = 0.015625


def runs(columns):
    out = []
    for j in sorted(columns):
        if out and out[-1][0] + out[-1][1] == j:
            out[-1] = (out[-1][0], out[-1][1] + 1)
        else:
            out.append((j, 1))
    return out


def receive_plan(half, parity):
    band = 2 * half + 1
    own = (half, half + 1)
    partner = 1 - 2 * parity
    owned = {}
    for i in range(band + 1):
        for j in range(i, band + 1):
            if j - i > half or i in own or j in own:
                continue
            chips = {i // 2 - half // 2, j // 2 - half // 2}
            rank = lambda e: (e != partner, e % 2 != 0, abs(e))
            owned.setdefault(min(chips, key=rank), []).append((i, j))
    plan = {}
    for e, pairs in owned.items():
        low = 2 * e + half
        options = []
        for pick in (0, 1):
            rows = {low: set(), low + 1: set()}
            for i, j in pairs:
                if i in rows and j in rows:
                    row = (i, j)[pick]
                    rows[row].add(i + j - row)
                elif i in rows:
                    rows[i].add(j)
                else:
                    rows[j].add(i)
            options.append({p: runs(c) for p, c in rows.items()})
        best = min(options, key=lambda o: sum(len(v) for v in o.values()))
        for p, v in best.items():
            plan[e, p] = v
    return plan


def kernel(ncol, n, b, half, margin, fock, density, kept, *rest):
    outs, rest = rest[:5], rest[5:]
    gd, gt, base, qd, qt = (o.at[0] for o in outs)
    (dw, fw, sw, tw, zrow, xrow, trow, dv, fv, mv, gm, cf, ch, co, present,
     lsem, wsend, wrecv, msend, mrecv) = rest
    band = 2 * half + 1
    r = lax.axis_index("row") * ncol + lax.axis_index("col")
    k = r // 2
    core = r % 2
    chips = n // 2
    parity = k % 2

    def device(t):
        return {"row": t // ncol, "col": t % ncol}

    def col(i, count=1):
        return pl.ds(pl.multiple_of(i * b, b), count * b)

    def valid_chip(e):
        return jnp.logical_and(k + e >= 0, k + e < chips)

    def valid(d):
        return jnp.logical_and(r + d >= 0, r + d < n)

    def both(x, y):
        return jnp.logical_and(x, y)

    sibling = device(r + 1 - 2 * core)
    offsets = [d for d in range(-half, half + 1) if d != 0]
    reach = half // 2
    hops = [e for m in range(reach, 0, -1) for e in (m, -m)]
    send_order = sorted(hops, key=abs)
    received = [receive_plan(half, q) for q in (0, 1)]
    near = 2
    spots = len(hops) + near

    loads = [
        pltpu.make_async_copy(density.at[0], dv, lsem.at[0]),
        pltpu.make_async_copy(fock.at[0], fv, lsem.at[1]),
        pltpu.make_async_copy(margin.at[0], mv, lsem.at[2]),
        pltpu.make_async_copy(kept, present, lsem.at[3]),
    ]
    for c in loads:
        c.start()

    barrier = pltpu.get_barrier_semaphore()
    for d in offsets:
        @pl.when(valid(d))
        def _():
            pl.semaphore_signal(barrier, inc=1, device_id=device(r + d),
                                device_id_type=pl.DeviceIdType.MESH)

    for e in hops:
        @pl.when(jnp.logical_not(valid_chip(e)))
        def _():
            p = half + 2 * e
            for w in (dw, fw, sw, tw):
                w[p * b:(p + 2) * b, :] = jnp.zeros((2 * b, w.shape[1]), w.dtype)
    for d in offsets:
        @pl.when(jnp.logical_not(valid(-d)))
        def _():
            for m in range(gm.shape[0]):
                gm[m, half - d] = jnp.zeros((b, b), gm.dtype)

    expected = jnp.minimum(r, half) + jnp.minimum(n - 1 - r, half)
    pl.semaphore_wait(barrier, expected)

    pending = []

    flights = []

    def reflect(w, sign, own_rows):
        middle = (half, half + 1)
        for q in (0, 1):
            known = {(p, j) for (_, p), v in received[q].items() for lo, count in v
                     for j in range(lo, lo + count)}
            todo = [(i, j) for i in range(band + 1) for j in range(band + 1)
                    if abs(i - j) <= half and i not in middle and (i, j) not in known
                    and (j in middle) == own_rows]

            def fill(todo=todo):
                for i, j in todo:
                    block = w[j * b:(j + 1) * b, (i + 1) * b:(i + 2) * b].T
                    w[i * b:(i + 1) * b, (j + 1) * b:(j + 2) * b] = block if sign > 0 else -block

            if own_rows:
                fill()
                return
            pl.when(parity == q)(fill)

    def spread_plan(phase, own, w):
        here = pl.ds(pl.multiple_of((half + core) * b, b), b)
        share = pltpu.make_async_remote_copy(
            src_ref=own, dst_ref=w.at[here, col(core + 1, band)],
            send_sem=wsend.at[phase, 0], recv_sem=wrecv.at[phase, 0],
            device_id=sibling, device_id_type=pl.DeviceIdType.MESH)
        moves = []
        for a, e in enumerate(hops):
            for q in (0, 1):
                for cc in (0, 1):
                    p = half - 2 * e + cc
                    for u, (lo, count) in enumerate(received[q].get((-e, p), [])):
                        slot = 1 + a + (len(hops) - near) * u
                        spot = w.at[p * b:(p + 1) * b, (lo + 1) * b:(lo + 1 + count) * b]
                        s0 = lo - p + half
                        send = pltpu.make_async_remote_copy(
                            src_ref=own.at[:, s0 * b:(s0 + count) * b], dst_ref=spot,
                            send_sem=wsend.at[phase, slot], recv_sem=wrecv.at[phase, slot],
                            device_id=device(r + 2 * e), device_id_type=pl.DeviceIdType.MESH)
                        relay = pltpu.make_async_remote_copy(
                            src_ref=spot, dst_ref=spot, send_sem=wsend.at[phase, spots + slot],
                            recv_sem=wrecv.at[phase, spots + slot], device_id=sibling,
                            device_id_type=pl.DeviceIdType.MESH)
                        moves.append((send, relay, e, q, cc, -e == 1 - 2 * q))
        return share, moves

    def spread_start(flight):
        for z in (0, 1):
            for cc in (0, 1):
                @pl.when(both(parity == z, core == cc))
                def _():
                    for send, _, e, q, c, partner in sorted(flight[1], key=lambda m: send_order.index(m[2])):
                        if (q + e) % 2 == z and c == cc:
                            if partner:
                                send.start()
                            else:
                                pl.when(valid_chip(e))(send.start)

    def spread_share(flight, w, own):
        here = pl.ds(pl.multiple_of((half + core) * b, b), b)
        flight[0].start()
        w[here, col(core + 1, band)] = own[...]

    def spread_finish(w, sign, flight):
        share, moves = flight
        share.wait_recv()
        reflect(w, sign, True)
        ordered = sorted(moves, key=lambda m: (not m[5], -abs(m[2])))
        for z in (0, 1):
            for cc in (0, 1):
                @pl.when(both(parity == z, core == cc))
                def _():
                    for send, relay, e, q, c, partner in ordered:
                        if q == z and c == cc:
                            def arrive():
                                send.wait_recv()
                                relay.start()
                            if partner:
                                arrive()
                            else:
                                pl.when(valid_chip(-e))(arrive)
                    for send, relay, e, q, c, partner in ordered:
                        if q == z and c == 1 - cc:
                            if partner:
                                relay.wait_recv()
                            else:
                                pl.when(valid_chip(-e))(relay.wait_recv)
        flights.append(flight)
        reflect(w, sign, False)

    def drain():
        for share, moves in flights:
            share.wait_send()
            for z in (0, 1):
                for cc in (0, 1):
                    @pl.when(both(parity == z, core == cc))
                    def _():
                        for send, relay, e, q, c, partner in moves:
                            if (q + e) % 2 == z and c == cc:
                                if partner:
                                    send.wait_send()
                                else:
                                    pl.when(valid_chip(e))(send.wait_send)
                            if q == z and c == cc:
                                if partner:
                                    relay.wait_send()
                                else:
                                    pl.when(valid_chip(-e))(relay.wait_send)
        flights.clear()
        for cond, c in pending:
            pl.when(cond)(c.wait_send)
        pending.clear()

    def mirror(phase, left, w, own, m):
        copies = []
        for i, d in enumerate(sorted(offsets, key=lambda v: -abs(v))):
            product(left, w, own, (half + d,))
            c = pltpu.make_async_remote_copy(
                src_ref=own.at[:, (half + d) * b:(half + d + 1) * b],
                dst_ref=m.at[half - d], send_sem=msend.at[phase, i],
                recv_sem=mrecv.at[phase, i], device_id=device(r + d),
                device_id_type=pl.DeviceIdType.MESH)

            @pl.when(valid(d))
            def _():
                c.start()
            copies.append((d, c))
        product(left, w, own, (half,))
        m[half] = own[:, half * b:(half + 1) * b]
        for d, c in copies:
            pending.append((valid(d), c))
        return copies

    def mirror_use(copies, use):
        for d, c in copies:
            pl.when(valid(-d))(c.wait_recv)
        for o in range(-half, half + 1):
            use(o)

    def product(left, w, out, columns=None):
        for c in columns or range(band):
            lo, hi = max(0, c - half), min(band, c + half + 1)
            rhs = w[pl.ds(pl.multiple_of((core + lo) * b, b), (hi - lo) * b), col(core + 1 + c)]
            acc = jnp.dot(left[:, lo * b:hi * b], rhs, preferred_element_type=jnp.float32)
            keep = present[0, c].astype(jnp.float32)
            out[:, c * b:(c + 1) * b] = (acc * keep).astype(out.dtype)

    def columns(o):
        return slice((half + o) * b, (half + o + 1) * b)

    def gradient(o):
        other = gm[0, half + o].T
        gt[:, columns(o)] = other
        g = other.astype(jnp.float32) - gd[:, columns(o)].astype(jnp.float32)
        trow[:, columns(o)] = (-STEP_SCALE * g).astype(trow.dtype)

    def commute(o):
        v = cf[:, columns(o)].astype(jnp.float32) + gm[1, half + o].T.astype(jnp.float32)
        ch[:, columns(o)] = v.astype(ch.dtype)
        base[:, columns(o)] = dv[:, columns(o)].astype(jnp.float32) + v

    def second(o):
        qt[:, columns(o)] = gm[2, half + o].T

    def body():
        dflight, fflight = spread_plan(0, dv, dw), spread_plan(1, fv, fw)
        sflight, tflight = spread_plan(2, mv, sw), spread_plan(0, trow, tw)
        loads[0].wait()
        spread_start(dflight)
        spread_share(dflight, dw, dv)
        loads[1].wait()
        spread_start(fflight)
        spread_share(fflight, fw, fv)
        loads[2].wait()
        loads[3].wait()
        spread_finish(dw, 1, dflight)
        spread_start(sflight)
        spread_share(sflight, sw, mv)
        product(mv, dw, zrow)
        spread_finish(fw, 1, fflight)
        copies = mirror(0, zrow, fw, gd, gm.at[0])
        spread_finish(sw, 1, sflight)
        product(dv, sw, xrow)
        mirror_use(copies, gradient)
        drain()
        spread_start(tflight)
        spread_share(tflight, tw, trow)
        spread_finish(tw, -1, tflight)
        copies = mirror(1, xrow, tw, cf, gm.at[1])
        mirror_use(copies, commute)
        drain()
        product(ch, sw, co)
        copies = mirror(0, co, tw, qd, gm.at[2])
        mirror_use(copies, second)

    body()
    drain()


def local(ncol, n, margin, fock_matrix, density, present):
    rows, b, width = margin.shape
    band = present.shape[1]
    half = (band - 1) // 2
    bf = jnp.bfloat16
    row = pltpu.VMEM((b, width), bf)
    wide = pltpu.VMEM(((band + 1) * b, (band + 3) * b), bf)
    out = jax.ShapeDtypeStruct((rows, b, width), bf)
    outs = pl.pallas_call(
        functools.partial(kernel, ncol, n, b, half),
        out_shape=(out, out, jax.ShapeDtypeStruct((rows, b, width), jnp.float32), out, out),
        in_specs=[pl.BlockSpec(memory_space=pltpu.HBM)] * 4,
        out_specs=[pl.BlockSpec(memory_space=pltpu.VMEM)] * 5,
        scratch_shapes=[
            wide, wide, wide, wide, row, row, row, row, row, row,
            pltpu.VMEM((3, band, b, b), bf), row, row, row, pltpu.SMEM((rows, band), jnp.int32),
            pltpu.SemaphoreType.DMA((4,)),
            pltpu.SemaphoreType.DMA((3, 5 + 2 * half)),
            pltpu.SemaphoreType.DMA((3, 5 + 2 * half)),
            pltpu.SemaphoreType.DMA((2, 2 * half)),
            pltpu.SemaphoreType.DMA((2, 2 * half)),
        ],
        compiler_params=pltpu.CompilerParams(
            collective_id=0, has_side_effects=True, vmem_limit_bytes=30000000),
        name="density_step",
    )(*(pltpu.with_memory_space_constraint(v, pltpu.HBM) for v in (margin, fock_matrix, density, present)))
    gd, gt, base, qd, qt = (v.astype(jnp.float32) for v in outs)
    return gt - gd, base + 0.5 * (qd + qt)


def solution(mesh):
    nrow, ncol = mesh.shape["row"], mesh.shape["col"]
    spec3 = P(("row", "col"), None, None)
    return jax.shard_map(
        functools.partial(local, ncol, nrow * ncol), mesh=mesh,
        in_specs=(spec3, spec3, spec3, P(("row", "col"), None)),
        out_specs=(spec3, spec3), check_vma=False)
```

```python
import functools

import jax
import jax.numpy as jnp
from jax import lax
from jax.experimental import pallas as pl
from jax.experimental.pallas import tpu as pltpu
from jax.sharding import PartitionSpec as P

STEP_SCALE = 0.015625


def runs(columns):
    out = []
    for j in sorted(columns):
        if out and out[-1][0] + out[-1][1] == j:
            out[-1] = (out[-1][0], out[-1][1] + 1)
        else:
            out.append((j, 1))
    return out


def receive_plan(half, parity):
    band = 2 * half + 1
    own = (half, half + 1)
    partner = 1 - 2 * parity
    owned = {}
    for i in range(band + 1):
        for j in range(i, band + 1):
            if j - i > half or i in own or j in own:
                continue
            chips = {i // 2 - half // 2, j // 2 - half // 2}
            rank = lambda e: (e != partner, e % 2 != 0, abs(e))
            owned.setdefault(min(chips, key=rank), []).append((i, j))
    plan = {}
    for e, pairs in owned.items():
        low = 2 * e + half
        options = []
        for pick in (0, 1):
            rows = {low: set(), low + 1: set()}
            for i, j in pairs:
                if i in rows and j in rows:
                    row = (i, j)[pick]
                    rows[row].add(i + j - row)
                elif i in rows:
                    rows[i].add(j)
                else:
                    rows[j].add(i)
            options.append({p: runs(c) for p, c in rows.items()})
        best = min(options, key=lambda o: sum(len(v) for v in o.values()))
        for p, v in best.items():
            plan[e, p] = v
    return plan


def kernel(ncol, n, b, half, margin, fock, density, kept, *rest):
    outs, rest = rest[:5], rest[5:]
    gd, gt, base, qd, qt = (o.at[0] for o in outs)
    (dw, fw, sw, tw, zrow, xrow, trow, dv, fv, mv, gm, cf, ch, co, present,
     lsem, wsend, wrecv, msend, mrecv) = rest
    band = 2 * half + 1
    r = lax.axis_index("row") * ncol + lax.axis_index("col")
    k = r // 2
    core = r % 2
    chips = n // 2
    parity = k % 2

    def device(t):
        return {"row": t // ncol, "col": t % ncol}

    def col(i, count=1):
        return pl.ds(pl.multiple_of(i * b, b), count * b)

    def valid_chip(e):
        return jnp.logical_and(k + e >= 0, k + e < chips)

    def valid(d):
        return jnp.logical_and(r + d >= 0, r + d < n)

    def both(x, y):
        return jnp.logical_and(x, y)

    sibling = device(r + 1 - 2 * core)
    offsets = [d for d in range(-half, half + 1) if d != 0]
    reach = half // 2
    hops = [e for m in range(reach, 0, -1) for e in (m, -m)]
    received = [receive_plan(half, q) for q in (0, 1)]
    near = 2
    spots = len(hops) + near

    loads = [
        pltpu.make_async_copy(density.at[0], dv, lsem.at[0]),
        pltpu.make_async_copy(fock.at[0], fv, lsem.at[1]),
        pltpu.make_async_copy(margin.at[0], mv, lsem.at[2]),
        pltpu.make_async_copy(kept, present, lsem.at[3]),
    ]
    for c in loads:
        c.start()

    barrier = pltpu.get_barrier_semaphore()
    for d in offsets:
        @pl.when(valid(d))
        def _():
            pl.semaphore_signal(barrier, inc=1, device_id=device(r + d),
                                device_id_type=pl.DeviceIdType.MESH)

    for e in hops:
        @pl.when(jnp.logical_not(valid_chip(e)))
        def _():
            p = half + 2 * e
            for w in (dw, fw, sw, tw):
                w[p * b:(p + 2) * b, :] = jnp.zeros((2 * b, w.shape[1]), w.dtype)
    for d in offsets:
        @pl.when(jnp.logical_not(valid(-d)))
        def _():
            for m in range(gm.shape[0]):
                gm[m, half - d] = jnp.zeros((b, b), gm.dtype)

    expected = jnp.minimum(r, half) + jnp.minimum(n - 1 - r, half)
    pl.semaphore_wait(barrier, expected)

    pending = []

    flights = []

    def reflect(w, sign, own_rows):
        middle = (half, half + 1)
        for q in (0, 1):
            known = {(p, j) for (_, p), v in received[q].items() for lo, count in v
                     for j in range(lo, lo + count)}
            todo = [(i, j) for i in range(band + 1) for j in range(band + 1)
                    if abs(i - j) <= half and i not in middle and (i, j) not in known
                    and (j in middle) == own_rows]

            def fill(todo=todo):
                for i, j in todo:
                    block = w[j * b:(j + 1) * b, (i + 1) * b:(i + 2) * b].T
                    w[i * b:(i + 1) * b, (j + 1) * b:(j + 2) * b] = block if sign > 0 else -block

            if own_rows:
                fill()
                return
            pl.when(parity == q)(fill)

    def spread_plan(phase, own, w):
        here = pl.ds(pl.multiple_of((half + core) * b, b), b)
        share = pltpu.make_async_remote_copy(
            src_ref=own, dst_ref=w.at[here, col(core + 1, band)],
            send_sem=wsend.at[phase, 0], recv_sem=wrecv.at[phase, 0],
            device_id=sibling, device_id_type=pl.DeviceIdType.MESH)
        moves = []
        for a, e in enumerate(hops):
            for q in (0, 1):
                for cc in (0, 1):
                    p = half - 2 * e + cc
                    for u, (lo, count) in enumerate(received[q].get((-e, p), [])):
                        slot = 1 + a + (len(hops) - near) * u
                        spot = w.at[p * b:(p + 1) * b, (lo + 1) * b:(lo + 1 + count) * b]
                        s0 = lo - p + half
                        send = pltpu.make_async_remote_copy(
                            src_ref=own.at[:, s0 * b:(s0 + count) * b], dst_ref=spot,
                            send_sem=wsend.at[phase, slot], recv_sem=wrecv.at[phase, slot],
                            device_id=device(r + 2 * e), device_id_type=pl.DeviceIdType.MESH)
                        relay = pltpu.make_async_remote_copy(
                            src_ref=spot, dst_ref=spot, send_sem=wsend.at[phase, spots + slot],
                            recv_sem=wrecv.at[phase, spots + slot], device_id=sibling,
                            device_id_type=pl.DeviceIdType.MESH)
                        moves.append((send, relay, e, q, cc, -e == 1 - 2 * q))
        return share, moves

    def far_first(move):
        return move[5], abs(move[2])

    def spread_start(flight, key):
        for z in (0, 1):
            for cc in (0, 1):
                @pl.when(both(parity == z, core == cc))
                def _():
                    for send, _, e, q, c, partner in sorted(flight[1], key=key):
                        if (q + e) % 2 == z and c == cc:
                            if partner:
                                send.start()
                            else:
                                pl.when(valid_chip(e))(send.start)

    def spread_share(flight, w, own):
        here = pl.ds(pl.multiple_of((half + core) * b, b), b)
        flight[0].start()
        w[here, col(core + 1, band)] = own[...]

    def spread_finish(w, sign, flight):
        share, moves = flight
        share.wait_recv()
        reflect(w, sign, True)
        ordered = sorted(moves, key=lambda m: (not m[5], -abs(m[2])))
        for z in (0, 1):
            for cc in (0, 1):
                @pl.when(both(parity == z, core == cc))
                def _():
                    for send, relay, e, q, c, partner in ordered:
                        if q == z and c == cc:
                            def arrive():
                                send.wait_recv()
                                relay.start()
                            if partner:
                                arrive()
                            else:
                                pl.when(valid_chip(-e))(arrive)
                    for send, relay, e, q, c, partner in ordered:
                        if q == z and c == 1 - cc:
                            if partner:
                                relay.wait_recv()
                            else:
                                pl.when(valid_chip(-e))(relay.wait_recv)
        flights.append(flight)
        reflect(w, sign, False)

    def drain(mirrored):
        for share, moves in flights:
            share.wait_send()
            for z in (0, 1):
                for cc in (0, 1):
                    @pl.when(both(parity == z, core == cc))
                    def _():
                        for send, relay, e, q, c, partner in moves:
                            if (q + e) % 2 == z and c == cc:
                                if partner:
                                    send.wait_send()
                                else:
                                    pl.when(valid_chip(e))(send.wait_send)
                            if q == z and c == cc:
                                if partner:
                                    relay.wait_send()
                                else:
                                    pl.when(valid_chip(-e))(relay.wait_send)
        flights.clear()
        for cond, c in mirrored:
            pl.when(cond)(c.wait_send)

    def mirror(phase, left, w, own, m):
        copies = []
        for i, d in enumerate(sorted(offsets, key=lambda v: -abs(v))):
            product(left, w, own, (half + d,))
            c = pltpu.make_async_remote_copy(
                src_ref=own.at[:, (half + d) * b:(half + d + 1) * b],
                dst_ref=m.at[half - d], send_sem=msend.at[phase, i],
                recv_sem=mrecv.at[phase, i], device_id=device(r + d),
                device_id_type=pl.DeviceIdType.MESH)

            @pl.when(valid(d))
            def _():
                c.start()
            copies.append((d, c))
        product(left, w, own, (half,))
        m[half] = own[:, half * b:(half + 1) * b]
        for d, c in copies:
            pending.append((valid(d), c))
        return copies

    def mirror_use(copies, use):
        for d, c in copies:
            pl.when(valid(-d))(c.wait_recv)
        for o in range(-half, half + 1):
            use(o)

    def product(left, w, out, columns=None):
        for c in columns or range(band):
            lo, hi = max(0, c - half), min(band, c + half + 1)
            rhs = w[pl.ds(pl.multiple_of((core + lo) * b, b), (hi - lo) * b), col(core + 1 + c)]
            acc = jnp.dot(left[:, lo * b:hi * b], rhs, preferred_element_type=jnp.float32)
            keep = present[0, c].astype(jnp.float32)
            out[:, c * b:(c + 1) * b] = (acc * keep).astype(out.dtype)

    def columns(o):
        return slice((half + o) * b, (half + o + 1) * b)

    def gradient(o):
        other = gm[0, half + o].T
        gt[:, columns(o)] = other
        g = other.astype(jnp.float32) - gd[:, columns(o)].astype(jnp.float32)
        trow[:, columns(o)] = (-STEP_SCALE * g).astype(trow.dtype)

    def commute(o):
        v = cf[:, columns(o)].astype(jnp.float32) + gm[1, half + o].T.astype(jnp.float32)
        ch[:, columns(o)] = v.astype(ch.dtype)
        base[:, columns(o)] = dv[:, columns(o)].astype(jnp.float32) + v

    def second(o):
        qt[:, columns(o)] = gm[2, half + o].T

    def body():
        dflight, fflight = spread_plan(0, dv, dw), spread_plan(1, fv, fw)
        sflight, tflight = spread_plan(2, mv, sw), spread_plan(0, trow, tw)
        loads[0].wait()
        spread_start(dflight, far_first)
        spread_share(dflight, dw, dv)
        loads[1].wait()
        spread_start(fflight, far_first)
        loads[2].wait()
        loads[3].wait()
        spread_finish(dw, 1, dflight)
        spread_share(fflight, fw, fv)
        spread_start(sflight, far_first)
        spread_share(sflight, sw, mv)
        product(mv, dw, zrow)
        spread_finish(fw, 1, fflight)
        copies = mirror(0, zrow, fw, gd, gm.at[0])
        spread_finish(sw, 1, sflight)
        product(dv, sw, xrow)
        drain([])
        mirror_use(copies, gradient)
        spread_start(tflight, far_first)
        spread_share(tflight, tw, trow)
        spread_finish(tw, -1, tflight)
        earlier = list(pending)
        pending.clear()
        copies = mirror(1, xrow, tw, cf, gm.at[1])
        drain(earlier)
        mirror_use(copies, commute)
        product(ch, sw, co)
        copies = mirror(0, co, tw, qd, gm.at[2])
        mirror_use(copies, second)

    body()
    drain(pending)


def local(ncol, n, margin, fock_matrix, density, present):
    rows, b, width = margin.shape
    band = present.shape[1]
    half = (band - 1) // 2
    bf = jnp.bfloat16
    row = pltpu.VMEM((b, width), bf)
    wide = pltpu.VMEM(((band + 1) * b, (band + 3) * b), bf)
    out = jax.ShapeDtypeStruct((rows, b, width), bf)
    outs = pl.pallas_call(
        functools.partial(kernel, ncol, n, b, half),
        out_shape=(out, out, jax.ShapeDtypeStruct((rows, b, width), jnp.float32), out, out),
        in_specs=[pl.BlockSpec(memory_space=pltpu.HBM)] * 4,
        out_specs=[pl.BlockSpec(memory_space=pltpu.VMEM)] * 5,
        scratch_shapes=[
            wide, wide, wide, wide, row, row, row, row, row, row,
            pltpu.VMEM((3, band, b, b), bf), row, row, row, pltpu.SMEM((rows, band), jnp.int32),
            pltpu.SemaphoreType.DMA((4,)),
            pltpu.SemaphoreType.DMA((3, 5 + 2 * half)),
            pltpu.SemaphoreType.DMA((3, 5 + 2 * half)),
            pltpu.SemaphoreType.DMA((2, 2 * half)),
            pltpu.SemaphoreType.DMA((2, 2 * half)),
        ],
        compiler_params=pltpu.CompilerParams(
            collective_id=0, has_side_effects=True, vmem_limit_bytes=30000000),
        name="density_step",
    )(*(pltpu.with_memory_space_constraint(v, pltpu.HBM) for v in (margin, fock_matrix, density, present)))
    gd, gt, base, qd, qt = (v.astype(jnp.float32) for v in outs)
    return gt - gd, base + 0.5 * (qd + qt)


def solution(mesh):
    nrow, ncol = mesh.shape["row"], mesh.shape["col"]
    spec3 = P(("row", "col"), None, None)
    return jax.shard_map(
        functools.partial(local, ncol, nrow * ncol), mesh=mesh,
        in_specs=(spec3, spec3, spec3, P(("row", "col"), None)),
        out_specs=(spec3, spec3), check_vma=False)
```

```python
import functools

import jax
import jax.numpy as jnp
from jax import lax
from jax.experimental import pallas as pl
from jax.experimental.pallas import tpu as pltpu
from jax.sharding import PartitionSpec as P

STEP_SCALE = 0.015625


def runs(columns):
    out = []
    for j in sorted(columns):
        if out and out[-1][0] + out[-1][1] == j:
            out[-1] = (out[-1][0], out[-1][1] + 1)
        else:
            out.append((j, 1))
    return out


def receive_plan(half, parity):
    band = 2 * half + 1
    own = (half, half + 1)
    partner = 1 - 2 * parity
    owned = {}
    for i in range(band + 1):
        for j in range(i, band + 1):
            if j - i > half or i in own or j in own:
                continue
            chips = {i // 2 - half // 2, j // 2 - half // 2}
            rank = lambda e: (e != partner, e % 2 != 0, abs(e))
            owned.setdefault(min(chips, key=rank), []).append((i, j))
    plan = {}
    for e, pairs in owned.items():
        low = 2 * e + half
        options = []
        for pick in (0, 1):
            rows = {low: set(), low + 1: set()}
            for i, j in pairs:
                if i in rows and j in rows:
                    row = (i, j)[pick]
                    rows[row].add(i + j - row)
                elif i in rows:
                    rows[i].add(j)
                else:
                    rows[j].add(i)
            options.append({p: runs(c) for p, c in rows.items()})
        best = min(options, key=lambda o: sum(len(v) for v in o.values()))
        for p, v in best.items():
            plan[e, p] = v
    return plan


def kernel(ncol, n, b, half, margin, fock, density, kept, *rest):
    outs, rest = rest[:5], rest[5:]
    gd, gt, base, qd, qt = (o.at[0] for o in outs)
    (dw, fw, sw, tw, zrow, xrow, trow, dv, fv, mv, gm, cf, ch, co, present,
     lsem, wsend, wrecv, msend, mrecv) = rest
    band = 2 * half + 1
    r = lax.axis_index("row") * ncol + lax.axis_index("col")
    k = r // 2
    core = r % 2
    chips = n // 2
    parity = k % 2

    def device(t):
        return {"row": t // ncol, "col": t % ncol}

    def col(i, count=1):
        return pl.ds(pl.multiple_of(i * b, b), count * b)

    def valid_chip(e):
        return jnp.logical_and(k + e >= 0, k + e < chips)

    def valid(d):
        return jnp.logical_and(r + d >= 0, r + d < n)

    def both(x, y):
        return jnp.logical_and(x, y)

    sibling = device(r + 1 - 2 * core)
    offsets = [d for d in range(-half, half + 1) if d != 0]
    reach = half // 2
    hops = [e for m in range(reach, 0, -1) for e in (m, -m)]
    received = [receive_plan(half, q) for q in (0, 1)]
    near = 2
    spots = len(hops) + near

    loads = [
        pltpu.make_async_copy(density.at[0], dv, lsem.at[0]),
        pltpu.make_async_copy(fock.at[0], fv, lsem.at[1]),
        pltpu.make_async_copy(margin.at[0], mv, lsem.at[2]),
        pltpu.make_async_copy(kept, present, lsem.at[3]),
    ]
    for c in loads:
        c.start()

    barrier = pltpu.get_barrier_semaphore()
    for d in offsets:
        @pl.when(valid(d))
        def _():
            pl.semaphore_signal(barrier, inc=1, device_id=device(r + d),
                                device_id_type=pl.DeviceIdType.MESH)

    for e in hops:
        @pl.when(jnp.logical_not(valid_chip(e)))
        def _():
            p = half + 2 * e
            for w in (dw, fw, sw, tw):
                w[p * b:(p + 2) * b, :] = jnp.zeros((2 * b, w.shape[1]), w.dtype)
    for d in offsets:
        @pl.when(jnp.logical_not(valid(-d)))
        def _():
            for m in range(gm.shape[0]):
                gm[m, half - d] = jnp.zeros((b, b), gm.dtype)

    expected = jnp.minimum(r, half) + jnp.minimum(n - 1 - r, half)
    pl.semaphore_wait(barrier, expected)

    pending = []

    flights = []

    def reflect(w, sign, own_rows):
        middle = (half, half + 1)
        for q in (0, 1):
            known = {(p, j) for (_, p), v in received[q].items() for lo, count in v
                     for j in range(lo, lo + count)}
            todo = [(i, j) for i in range(band + 1) for j in range(band + 1)
                    if abs(i - j) <= half and i not in middle and (i, j) not in known
                    and (j in middle) == own_rows]

            def fill(todo=todo):
                for i, j in todo:
                    block = w[j * b:(j + 1) * b, (i + 1) * b:(i + 2) * b].T
                    w[i * b:(i + 1) * b, (j + 1) * b:(j + 2) * b] = block if sign > 0 else -block

            if own_rows:
                fill()
                return
            pl.when(parity == q)(fill)

    def spread_plan(phase, own, w):
        here = pl.ds(pl.multiple_of((half + core) * b, b), b)
        share = pltpu.make_async_remote_copy(
            src_ref=own, dst_ref=w.at[here, col(core + 1, band)],
            send_sem=wsend.at[phase, 0], recv_sem=wrecv.at[phase, 0],
            device_id=sibling, device_id_type=pl.DeviceIdType.MESH)
        moves = []
        for a, e in enumerate(hops):
            for q in (0, 1):
                for cc in (0, 1):
                    p = half - 2 * e + cc
                    for u, (lo, count) in enumerate(received[q].get((-e, p), [])):
                        slot = 1 + a + (len(hops) - near) * u
                        spot = w.at[p * b:(p + 1) * b, (lo + 1) * b:(lo + 1 + count) * b]
                        s0 = lo - p + half
                        send = pltpu.make_async_remote_copy(
                            src_ref=own.at[:, s0 * b:(s0 + count) * b], dst_ref=spot,
                            send_sem=wsend.at[phase, slot], recv_sem=wrecv.at[phase, slot],
                            device_id=device(r + 2 * e), device_id_type=pl.DeviceIdType.MESH)
                        relay = pltpu.make_async_remote_copy(
                            src_ref=spot, dst_ref=spot, send_sem=wsend.at[phase, spots + slot],
                            recv_sem=wrecv.at[phase, spots + slot], device_id=sibling,
                            device_id_type=pl.DeviceIdType.MESH)
                        moves.append((send, relay, e, q, cc, -e == 1 - 2 * q))
        return share, moves

    def far_first(move):
        return move[5], abs(move[2])

    def spread_start(flight, key):
        for z in (0, 1):
            for cc in (0, 1):
                @pl.when(both(parity == z, core == cc))
                def _():
                    for send, _, e, q, c, partner in sorted(flight[1], key=key):
                        if (q + e) % 2 == z and c == cc:
                            if partner:
                                send.start()
                            else:
                                pl.when(valid_chip(e))(send.start)

    def spread_share(flight, w, own):
        here = pl.ds(pl.multiple_of((half + core) * b, b), b)
        flight[0].start()
        w[here, col(core + 1, band)] = own[...]

    def spread_finish(w, sign, flight):
        share, moves = flight
        share.wait_recv()
        reflect(w, sign, True)
        ordered = sorted(moves, key=lambda m: (not m[5], -abs(m[2])))
        for z in (0, 1):
            for cc in (0, 1):
                @pl.when(both(parity == z, core == cc))
                def _():
                    for send, relay, e, q, c, partner in ordered:
                        if q == z and c == cc:
                            def arrive():
                                send.wait_recv()
                                relay.start()
                            if partner:
                                arrive()
                            else:
                                pl.when(valid_chip(-e))(arrive)
                    for send, relay, e, q, c, partner in ordered:
                        if q == z and c == 1 - cc:
                            if partner:
                                relay.wait_recv()
                            else:
                                pl.when(valid_chip(-e))(relay.wait_recv)
        flights.append(flight)
        reflect(w, sign, False)

    def drain(mirrored):
        for share, moves in flights:
            share.wait_send()
            for z in (0, 1):
                for cc in (0, 1):
                    @pl.when(both(parity == z, core == cc))
                    def _():
                        for send, relay, e, q, c, partner in moves:
                            if (q + e) % 2 == z and c == cc:
                                if partner:
                                    send.wait_send()
                                else:
                                    pl.when(valid_chip(e))(send.wait_send)
                            if q == z and c == cc:
                                if partner:
                                    relay.wait_send()
                                else:
                                    pl.when(valid_chip(-e))(relay.wait_send)
        flights.clear()
        for cond, c in mirrored:
            pl.when(cond)(c.wait_send)

    def mirror(phase, left, w, own, m):
        copies = []
        for i, d in enumerate(sorted(offsets, key=lambda v: -abs(v))):
            product(left, w, own, (half + d,))
            c = pltpu.make_async_remote_copy(
                src_ref=own.at[:, (half + d) * b:(half + d + 1) * b],
                dst_ref=m.at[half - d], send_sem=msend.at[phase, i],
                recv_sem=mrecv.at[phase, i], device_id=device(r + d),
                device_id_type=pl.DeviceIdType.MESH)

            @pl.when(valid(d))
            def _():
                c.start()
            copies.append((d, c))
        product(left, w, own, (half,))
        m[half] = own[:, half * b:(half + 1) * b]
        for d, c in copies:
            pending.append((valid(d), c))
        return copies

    def mirror_use(copies, use):
        for d, c in copies:
            pl.when(valid(-d))(c.wait_recv)
        for o in range(-half, half + 1):
            use(o)

    def product(left, w, out, columns=None):
        for c in columns or range(band):
            lo, hi = max(0, c - half), min(band, c + half + 1)
            rhs = w[pl.ds(pl.multiple_of((core + lo) * b, b), (hi - lo) * b), col(core + 1 + c)]
            acc = jnp.dot(left[:, lo * b:hi * b], rhs, preferred_element_type=jnp.float32)
            keep = present[0, c].astype(jnp.float32)
            out[:, c * b:(c + 1) * b] = (acc * keep).astype(out.dtype)

    def columns(o):
        return slice((half + o) * b, (half + o + 1) * b)

    def gradient(o):
        other = gm[0, half + o].T
        gt[:, columns(o)] = other
        g = other.astype(jnp.float32) - gd[:, columns(o)].astype(jnp.float32)
        trow[:, columns(o)] = (-STEP_SCALE * g).astype(trow.dtype)

    def commute(o):
        v = cf[:, columns(o)].astype(jnp.float32) + gm[1, half + o].T.astype(jnp.float32)
        ch[:, columns(o)] = v.astype(ch.dtype)
        base[:, columns(o)] = dv[:, columns(o)].astype(jnp.float32) + v

    def second(o):
        qt[:, columns(o)] = gm[2, half + o].T

    def body():
        dflight, fflight = spread_plan(0, dv, dw), spread_plan(1, fv, fw)
        sflight, tflight = spread_plan(2, mv, sw), spread_plan(0, trow, tw)
        loads[0].wait()
        spread_start(dflight, far_first)
        spread_share(dflight, dw, dv)
        loads[1].wait()
        spread_start(fflight, far_first)
        loads[2].wait()
        loads[3].wait()
        spread_finish(dw, 1, dflight)
        spread_share(fflight, fw, fv)
        spread_start(sflight, far_first)
        spread_share(sflight, sw, mv)
        product(mv, dw, zrow)
        spread_finish(fw, 1, fflight)
        copies = mirror(0, zrow, fw, gd, gm.at[0])
        spread_finish(sw, 1, sflight)
        product(dv, sw, xrow)
        drain([])
        mirror_use(copies, gradient)
        spread_start(tflight, far_first)
        spread_share(tflight, tw, trow)
        spread_finish(tw, -1, tflight)
        earlier = list(pending)
        pending.clear()
        copies = mirror(1, xrow, tw, cf, gm.at[1])
        drain(earlier)
        mirror_use(copies, commute)
        product(ch, sw, co)
        copies = mirror(0, co, tw, qd, gm.at[2])
        drain(pending)
        mirror_use(copies, second)

    body()


def local(ncol, n, margin, fock_matrix, density, present):
    rows, b, width = margin.shape
    band = present.shape[1]
    half = (band - 1) // 2
    bf = jnp.bfloat16
    row = pltpu.VMEM((b, width), bf)
    wide = pltpu.VMEM(((band + 1) * b, (band + 3) * b), bf)
    out = jax.ShapeDtypeStruct((rows, b, width), bf)
    outs = pl.pallas_call(
        functools.partial(kernel, ncol, n, b, half),
        out_shape=(out, out, jax.ShapeDtypeStruct((rows, b, width), jnp.float32), out, out),
        in_specs=[pl.BlockSpec(memory_space=pltpu.HBM)] * 4,
        out_specs=[pl.BlockSpec(memory_space=pltpu.VMEM)] * 5,
        scratch_shapes=[
            wide, wide, wide, wide, row, row, row, row, row, row,
            pltpu.VMEM((3, band, b, b), bf), row, row, row, pltpu.SMEM((rows, band), jnp.int32),
            pltpu.SemaphoreType.DMA((4,)),
            pltpu.SemaphoreType.DMA((3, 5 + 2 * half)),
            pltpu.SemaphoreType.DMA((3, 5 + 2 * half)),
            pltpu.SemaphoreType.DMA((2, 2 * half)),
            pltpu.SemaphoreType.DMA((2, 2 * half)),
        ],
        compiler_params=pltpu.CompilerParams(
            collective_id=0, has_side_effects=True, vmem_limit_bytes=30000000),
        name="density_step",
    )(*(pltpu.with_memory_space_constraint(v, pltpu.HBM) for v in (margin, fock_matrix, density, present)))
    gd, gt, base, qd, qt = (v.astype(jnp.float32) for v in outs)
    return gt - gd, base + 0.5 * (qd + qt)


def solution(mesh):
    nrow, ncol = mesh.shape["row"], mesh.shape["col"]
    spec3 = P(("row", "col"), None, None)
    return jax.shard_map(
        functools.partial(local, ncol, nrow * ncol), mesh=mesh,
        in_specs=(spec3, spec3, spec3, P(("row", "col"), None)),
        out_specs=(spec3, spec3), check_vma=False)
```
